512 devices in a mesh: dp: 8 (over x, core), seq: 64 (over y, z).
Axes of the slice: x: 4, y: 4, z: 16, core: 2. Of those that a mesh axis runs over, the one named last changes fastest.
Arguments:
- tokens: bfloat16 [131072, 512], P(('dp', 'seq')), parts along dimension 0, may hold values from -16 to 16
- globals_in: bfloat16 [1024, 512], P('dp'), parts along dimension 0, may hold values from -16 to 16
- seg_ids: int32 [131072], P(('dp', 'seq')), parts along dimension 0, may hold values from 1 to 63, as said below
- global_table: int32 [1024], P('dp'), parts along dimension 0, may hold values from 1 to 63
- w_qkv: bfloat16 [2, 512, 1536], replicated, may hold values from -1 to 1
- w_out: bfloat16 [2, 512, 512], replicated, may hold values from -0.25 to 0.25
- gain_local: float32 [2, 512], replicated, may hold values from 0.5 to 1.5
- gain_global: float32 [2, 512], replicated, may hold values from 0.5 to 1.5
- seg_bias: float32 [2, 8], replicated, may hold values from 2 to 5
Outputs:
- local_out: bfloat16 [131072, 512], P(('dp', 'seq')), parts along dimension 0
- global_out: bfloat16 [1024, 512], P('dp'), parts along dimension 0
The draws below stay inside these ranges and needn't reach their ends.
There are 8 independent parts, one for each index of `dp`. The reference program is written for one: setup_inputs(seed, part) draws one part's arguments, and reference() takes and returns one part's arrays. A program takes and returns all parts, laid end to end along the dimension named above; an argument that names none is the same for every part. Nothing has to cross between parts.
Inputs may be any that keep to these rules, and one draw needn't show every extreme that they name: `seg_ids`: the entity ids come in runs of 128 consecutive tokens (the first and last runs of a context are shorter).
All inputs are finite; a program needn't handle non-finite values.
Results may differ from the reference program's by a relative error of at most 0.006.
Values may be sent and summed in bfloat16 or wider, within the bound.
No kernel may reach another device: no remote copies, remote signals or barrier semaphores. Data moves between devices by JAX's collectives and lax.ppermute only.
A program may use at most 192 MiB of HBM per device.

```python
import math
import jax
import jax.numpy as jnp
from jax import lax

D = 512
H = 8
G = 128
RADIUS = 256
KEYS = 64
LAYERS = 2
TOK_DEV = 256
SEQ = 16384


def drawn_direction():
    phase = (jnp.arange(D, dtype=jnp.int32) * 37 % D).astype(jnp.float32)
    return math.sqrt(2.0) * jnp.cos(phase * (2.0 * math.pi / D) + 0.5)


def marked_rows(key, count, share):
    noise_key, mark_key, level_key = jax.random.split(key, 3)
    noise = jax.random.truncated_normal(noise_key, -6.0, 6.0, (count, D), jnp.float32)
    level = jax.random.uniform(level_key, (count, 1), jnp.float32, 1.5, 4.0)
    marked = jax.random.bernoulli(mark_key, share, (count, 1)).astype(jnp.float32)
    return noise + marked * level * drawn_direction()[None, :]


def draw_tokens(key, part):
    return marked_rows(jax.random.fold_in(key, 11), SEQ, 0.0625).astype(jnp.bfloat16)


def draw_globals_in(key, part):
    return marked_rows(jax.random.fold_in(key, 23), G, 0.25).astype(jnp.bfloat16)


def draw_seg_ids(key, part):
    run_length = max(RADIUS // 2, 1)
    run_count = SEQ // run_length + 1
    run_ids = jax.random.randint(jax.random.fold_in(key, 53), (run_count,), 1, KEYS, jnp.int32)
    which = (jnp.arange(SEQ, dtype=jnp.int32) + run_length // 2) // run_length
    return run_ids[which]


def draw_w_qkv(key, part):
    base_key = jax.random.fold_in(key, 37)
    base = jax.random.truncated_normal(base_key, -4.0, 4.0, (LAYERS, D, 3 * D), jnp.float32) / math.sqrt(D)
    head_size = D // H
    strength = math.sqrt(270.0 / math.sqrt(head_size))
    column = jnp.arange(D, dtype=jnp.int32)
    signs = jnp.where((column * 7 + column // 3) % 2 == 0, 1.0, -1.0).astype(jnp.float32)
    pattern = strength / D * drawn_direction()[:, None] * signs[None, :]
    plant = jnp.concatenate([pattern, pattern, jnp.zeros((D, D), jnp.float32)], axis=1)
    return (base + plant[None]).astype(jnp.bfloat16)


def with_ends(drawn, own_key, smallest, high):
    longest = drawn.shape.index(max(drawn.shape))
    spots = []
    for shift in (0, 1):
        where = [jax.random.randint(jax.random.fold_in(own_key, axis), (), 0, length) for axis, length in enumerate(drawn.shape)]
        where[longest] = (where[longest] + shift) % drawn.shape[longest]
        spots.append(tuple(where))
    return drawn.at[spots[0]].set(smallest).at[spots[1]].set(high)


def gaussian(own_key, shape, scale, reach, held_as=jnp.bfloat16):
    drawn = scale * jax.random.normal(own_key, shape, jnp.float32)
    return jnp.clip(drawn, min=-reach, max=reach).astype(held_as)


def setup_inputs(seed: int = 0, part: int = 0) -> dict:
    seeds = jax.random.split(jax.random.key(seed), 10)
    part_splits = jax.random.split(jax.random.fold_in(seeds[9], part), 10)
    tokens = draw_tokens(jax.random.fold_in(jax.random.fold_in(seeds[9], part), 71), part)
    globals_in = draw_globals_in(jax.random.fold_in(jax.random.fold_in(seeds[9], part), 71), part)
    seg_ids = draw_seg_ids(jax.random.fold_in(jax.random.fold_in(seeds[9], part), 71), part)
    global_table = with_ends(jax.random.randint(part_splits[3], (G,), 1, KEYS), jax.random.fold_in(part_splits[3], 1), 1, KEYS - 1).astype(jnp.int32)
    w_qkv = draw_w_qkv(jax.random.fold_in(seeds[9], 71), part)
    w_out = gaussian(seeds[5], (LAYERS, D, D), D ** -0.5, 0.25)
    gain_local = jnp.clip(1.0 + 0.1 * jax.random.normal(seeds[6], (LAYERS, D), jnp.float32), 0.5, 1.5)
    gain_global = jnp.clip(1.0 + 0.1 * jax.random.normal(seeds[7], (LAYERS, D), jnp.float32), 0.5, 1.5)
    seg_bias = jnp.clip(jax.random.uniform(seeds[8], (LAYERS, H), jnp.float32, 2.0, 5.0), 2.0, 5.0)
    return dict(tokens=tokens, globals_in=globals_in, seg_ids=seg_ids, global_table=global_table, w_qkv=w_qkv, w_out=w_out, gain_local=gain_local, gain_global=gain_global, seg_bias=seg_bias)


masked_fill = -1e+30

def layer_norm(values, gain):
    average = lax.optimization_barrier(jnp.mean(values, axis=-1, keepdims=True))
    centered = values - average
    variance = lax.optimization_barrier(jnp.mean(centered * centered, axis=-1, keepdims=True))
    return (centered * lax.rsqrt(variance + 1e-05) * gain).astype(jnp.bfloat16)

def window_attend(queries, keys_ext, values_ext, seg_rows, seg_ext, valid, gkeys, gvalues, bias, scaling):
    rows = queries.shape[0]
    span = keys_ext.shape[0]
    radius = (span - rows) // 2
    scores = jnp.einsum('thd,shd->hts', queries, keys_ext, preferred_element_type=jnp.float32) * scaling
    offset = jnp.arange(span, dtype=jnp.int32)[None, :] - radius - jnp.arange(rows, dtype=jnp.int32)[:, None]
    allowed = (jnp.abs(offset) <= radius) & valid[None, :]
    same = (seg_rows[:, None] == seg_ext[None, :]).astype(jnp.float32)
    scores = scores + bias[:, None, None] * same[None]
    scores = jnp.where(allowed[None], scores, masked_fill)
    gscores = jnp.einsum('thd,ghd->htg', queries, gkeys, preferred_element_type=jnp.float32) * scaling
    top = jnp.maximum(lax.optimization_barrier(jnp.max(scores, axis=-1)), lax.optimization_barrier(jnp.max(gscores, axis=-1)))
    probs = jnp.exp(scores - top[..., None])
    gprobs = jnp.exp(gscores - top[..., None])
    total = lax.optimization_barrier(jnp.sum(probs, axis=-1)) + lax.optimization_barrier(jnp.sum(gprobs, axis=-1))
    mixed = jnp.einsum('hts,shd->thd', probs.astype(jnp.bfloat16), values_ext, preferred_element_type=jnp.float32)
    mixed = mixed + jnp.einsum('htg,ghd->thd', gprobs.astype(jnp.bfloat16), gvalues, preferred_element_type=jnp.float32)
    return (mixed / jnp.transpose(total)[:, :, None]).reshape(rows, -1).astype(jnp.bfloat16)

def partial_global(gqueries, keys_loc, values_loc, seg_rows, table, scaling):
    scores = jnp.einsum('ghd,thd->ght', gqueries, keys_loc, preferred_element_type=jnp.float32) * scaling
    member = (table[:, None] == seg_rows[None, :])[:, None, :]
    scores = jnp.where(member, scores, masked_fill)
    top = lax.optimization_barrier(jnp.max(scores, axis=-1))
    probs = jnp.where(member, jnp.exp(scores - top[..., None]), jnp.float32(0.0))
    total = lax.optimization_barrier(jnp.sum(probs, axis=-1))
    weighted = jnp.einsum('ght,thd->ghd', probs, values_loc.astype(jnp.float32), precision=lax.Precision.HIGHEST)
    return (top, total, weighted)

def self_global(gqueries, gkeys, gvalues, scaling):
    scores = jnp.einsum('ghd,khd->ghk', gqueries, gkeys, preferred_element_type=jnp.float32) * scaling
    top = lax.optimization_barrier(jnp.max(scores, axis=-1))
    probs = jnp.exp(scores - top[..., None])
    total = lax.optimization_barrier(jnp.sum(probs, axis=-1))
    weighted = jnp.einsum('ghk,khd->ghd', probs, gvalues.astype(jnp.float32), precision=lax.Precision.HIGHEST)
    return (top, total, weighted)

def combine_parts(first, second):
    top = jnp.maximum(first[0], second[0])
    factor_a = jnp.exp(first[0] - top)
    factor_b = jnp.exp(second[0] - top)
    total = first[1] * factor_a + second[1] * factor_b
    weighted = first[2] * factor_a[..., None] + second[2] * factor_b[..., None]
    return (top, total, weighted)

def reference(tokens, globals_in, seg_ids, global_table, w_qkv, w_out, gain_local, gain_global, seg_bias):
    head_dim = D // H
    scaling = 1.0 / math.sqrt(head_dim)
    stream = tokens.astype(jnp.float32)
    gstate = globals_in.astype(jnp.float32)
    position = jnp.arange(SEQ + 2 * RADIUS, dtype=jnp.int32) - RADIUS
    valid_all = (position >= 0) & (position < SEQ)
    seg_padded = jnp.pad(seg_ids, (RADIUS, RADIUS), constant_values=-1)
    blocks = SEQ // TOK_DEV
    for layer_no in range(LAYERS):
        normed = layer_norm(stream, gain_local[layer_no])
        gnormed = layer_norm(gstate, gain_global[layer_no])
        proj = jnp.dot(normed, w_qkv[layer_no], preferred_element_type=jnp.float32).astype(jnp.bfloat16)
        gproj = jnp.dot(gnormed, w_qkv[layer_no], preferred_element_type=jnp.float32).astype(jnp.bfloat16)
        queries = proj[:, :D].reshape(SEQ, H, head_dim)
        keys_loc = proj[:, D:2 * D].reshape(SEQ, H, head_dim)
        values_loc = proj[:, 2 * D:].reshape(SEQ, H, head_dim)
        gqueries = gproj[:, :D].reshape(G, H, head_dim)
        gkeys = gproj[:, D:2 * D].reshape(G, H, head_dim)
        gvalues = gproj[:, 2 * D:].reshape(G, H, head_dim)
        keys_pad = jnp.pad(keys_loc, ((RADIUS, RADIUS), (0, 0), (0, 0)))
        values_pad = jnp.pad(values_loc, ((RADIUS, RADIUS), (0, 0), (0, 0)))
        bias = seg_bias[layer_no]

        def local_block(index):
            start = (index * TOK_DEV).astype(jnp.int32)
            span = TOK_DEV + 2 * RADIUS
            return window_attend(lax.dynamic_slice_in_dim(queries, start, TOK_DEV, 0), lax.dynamic_slice_in_dim(keys_pad, start, span, 0), lax.dynamic_slice_in_dim(values_pad, start, span, 0), lax.dynamic_slice_in_dim(seg_ids, start, TOK_DEV, 0), lax.dynamic_slice_in_dim(seg_padded, start, span, 0), lax.dynamic_slice_in_dim(valid_all, start, span, 0), gkeys, gvalues, bias, scaling)
        local_mix = lax.map(local_block, jnp.arange(blocks, dtype=jnp.int32)).reshape(SEQ, D)
        outer = partial_global(gqueries, keys_loc, values_loc, seg_ids, global_table, scaling)
        inner = self_global(gqueries, gkeys, gvalues, scaling)
        merged = combine_parts(outer, inner)
        global_mix = (merged[2] / merged[1][..., None]).reshape(G, D).astype(jnp.bfloat16)
        stream = stream + jnp.dot(local_mix, w_out[layer_no], preferred_element_type=jnp.float32)
        gstate = gstate + jnp.dot(global_mix, w_out[layer_no], preferred_element_type=jnp.float32)
    return (stream.astype(jnp.bfloat16), gstate.astype(jnp.bfloat16))
```

```python
import functools
import math

import jax
import jax.numpy as jnp
from jax import lax
from jax.experimental import pallas as pl
from jax.experimental.pallas import tpu as pltpu
from jax.sharding import PartitionSpec as P

RADIUS = 256
LAYERS = 2
LANES = 128
ENTITIES = 64
NEG = -1e30
BF16 = jnp.bfloat16
F32 = jnp.float32

VMEM = pl.BlockSpec(memory_space=pltpu.VMEM)
SMEM = pl.BlockSpec(memory_space=pltpu.SMEM)


def dot(a, b):
    return jnp.dot(a, b, preferred_element_type=F32)


def dot_nt(a, b):
    return lax.dot_general(a, b, (((1,), (1,)), ((), ())), preferred_element_type=F32)


def dot_tn(a, b):
    return lax.dot_general(a, b, (((0,), (0,)), ((), ())), preferred_element_type=F32)


def norm_rows(values, gain):
    average = jnp.mean(values, axis=-1, keepdims=True)
    centered = values - average
    variance = jnp.mean(centered * centered, axis=-1, keepdims=True)
    return (centered * lax.rsqrt(variance + 1e-05) * gain).astype(BF16)


def one_hot(ids):
    rows = lax.broadcasted_iota(jnp.int32, (ENTITIES, ids.shape[1]), 0)
    return jnp.where(rows == ids, 1.0, 0.0).astype(BF16)


def half_of(shape):
    return lax.broadcasted_iota(jnp.int32, shape, len(shape) - 1) // (LANES // 2)


def project(normed, w_ref, first, count, store):
    for tile in range(first, first + count, 2):
        part = dot(normed, w_ref[:, tile * LANES : (tile + 2) * LANES]).astype(BF16)
        store(tile, part[:, :LANES])
        store(tile + 1, part[:, LANES:])


def split_three(value):
    high = value.astype(BF16).astype(F32)
    rest = value - high
    middle = rest.astype(BF16).astype(F32)
    return high, middle, rest - middle


def partial_pair(gq, keys, vals, member):
    rows = gq.shape[0]
    half = half_of((rows, LANES))
    out = jnp.zeros((rows, LANES), F32)
    marks = jnp.zeros((rows, LANES), F32)
    lane = lax.broadcasted_iota(jnp.int32, (rows, LANES), 1)
    for head in range(2):
        query = jnp.where(half == head, gq, jnp.zeros_like(gq))
        scores = jnp.where(member, dot_nt(query, keys), NEG)
        top = jnp.max(scores, axis=-1, keepdims=True)
        probs = jnp.where(member, jnp.exp(scores - top), 0.0)
        total = jnp.sum(probs, axis=-1, keepdims=True)
        weighted = dot(probs.astype(BF16), vals)
        some = total > 0.0
        safe = jnp.where(some, total, 1.0)
        out = jnp.where(half == head, weighted / safe, out)
        lse = jnp.where(some, top + jnp.log(safe), NEG)
        for part, piece in enumerate(split_three(lse)):
            marks = jnp.where(lane == head + 2 * part, piece, marks)
    return out, marks


def store_payload(payload, pair, out, marks):
    both = jnp.concatenate(
        [out.reshape(-1, 8, LANES), marks.reshape(-1, 8, LANES)], axis=1
    )
    payload[pair] = both.astype(BF16)


def global_parts(gproj, kv_at, member, payload, pairs):
    def step(pair, carry):
        gq = gproj[pair] * jnp.asarray(0.125, BF16)
        out, marks = partial_pair(gq, kv_at(0, pair), kv_at(1, pair), member)
        store_payload(payload, pair, out, marks)
        return carry

    for pair in range(pairs):
        step(pair, 0)


def first_kernel(
    tokens, globals_in, seg, table, gain_l, gain_g, w_qkv, payload, gproj, kv
):
    pairs = payload.shape[0]
    gnormed = norm_rows(globals_in[...].astype(F32), gain_g[...])

    def put_g(tile, part):
        gproj[tile] = part

    project(gnormed, w_qkv, 0, 3 * pairs, put_g)
    normed = norm_rows(tokens[...].astype(F32), gain_l[...])

    def put_kv(tile, part):
        kv[tile - pairs] = part

    project(normed, w_qkv, pairs, 2 * pairs, put_kv)
    member = dot_tn(one_hot(table[...]), one_hot(seg[...])) > 0.5
    global_parts(gproj, lambda which, pair: kv[which * pairs + pair], member, payload, pairs)


def second_kernel(
    mix, gstate, seg, table, gain_g, w_out, w_qkv, kv, payload, gproj, gstate_next
):
    pairs = payload.shape[0]
    state = gstate[...].astype(F32)
    for pair in range(pairs):
        state = state + dot(mix[pair], w_out[pair * LANES : (pair + 1) * LANES, :])
    gstate_next[...] = state
    gnormed = norm_rows(state, gain_g[...])

    def put_g(tile, part):
        gproj[tile] = part

    project(gnormed, w_qkv, 0, 3 * pairs, put_g)
    member = dot_tn(one_hot(table[...]), one_hot(seg[...])) > 0.5
    global_parts(gproj, lambda which, pair: kv[which * pairs + pair], member, payload, pairs)


def combine_kernel(where, parts, gproj, out):
    peers = parts.shape[0]
    pairs = gproj.shape[0] // 3
    pair = where[0]
    row = pl.multiple_of(where[1] * 8, 8)
    gq = gproj[pair, pl.ds(row, 8), :] * jnp.asarray(0.125, BF16)
    gk = gproj[pairs + pair]
    gv = gproj[2 * pairs + pair]
    half = half_of((8, LANES))
    own = jnp.zeros((8, LANES), F32)
    own_lse = jnp.zeros((8, LANES), F32)
    for head in range(2):
        query = jnp.where(half == head, gq, jnp.zeros_like(gq))
        scores = dot_nt(query, gk)
        top = jnp.max(scores, axis=-1, keepdims=True)
        probs = jnp.exp(scores - top)
        total = jnp.sum(probs, axis=-1, keepdims=True)
        own = jnp.where(half == head, dot(probs.astype(BF16), gv) / total, own)
        own_lse = jnp.where(half == head, top + jnp.log(total), own_lse)
    lane = lax.broadcasted_iota(jnp.int32, (LANES, LANES), 0)
    spread = jnp.where((lane < 6) & (lane % 2 == half_of((LANES, LANES))), 1.0, 0.0)
    both = parts[...].astype(F32)
    marks = both[:, 8:, :].reshape(peers * 8, LANES).astype(BF16)
    lse = dot(marks, spread.astype(BF16)).reshape(peers, 8, LANES)
    top = jnp.maximum(jnp.max(lse, axis=0), own_lse)
    weight = jnp.exp(lse - top[None])
    own_weight = jnp.exp(own_lse - top)
    total = jnp.sum(weight, axis=0) + own_weight
    mixed = jnp.sum(weight * both[:, :8, :], axis=0) + own_weight * own
    result = (mixed / total).astype(BF16)
    out[...] = jnp.broadcast_to(result[None], out.shape)


def last_kernel(mix, gstate, w_out, out):
    state = gstate[...]
    for pair in range(mix.shape[0]):
        state = state + dot(mix[pair], w_out[pair * LANES : (pair + 1) * LANES, :])
    out[...] = state.astype(BF16)


def attend(bias, layer_no, gproj, seg_lo, seg, seg_hi, queries, keys, vals, same, neg, mixed):
    pairs = queries.shape[0]
    rows = queries.shape[1]
    tile = rows // 2
    span = same.shape[2]
    globals_count = gproj.shape[1]
    for pair in range(pairs):
        for which, ref in ((1, keys), (2, vals)):
            block = gproj[which * pairs + pair]
            ref[pair, :globals_count, :] = block
            ref[pair, globals_count + rows + 2 * RADIUS :, :] = block
    ext = jnp.concatenate([seg_lo[...], seg[...], seg_hi[...]], axis=1)
    hot = one_hot(ext)
    alike = dot_tn(one_hot(seg[...]), hot)
    valid = jnp.where(ext > 0, 0.0, NEG)
    i = lax.broadcasted_iota(jnp.int32, (rows, rows + 2 * RADIUS), 0)
    e = lax.broadcasted_iota(jnp.int32, (rows, rows + 2 * RADIUS), 1)
    barred = jnp.where((e >= i) & (e <= i + 2 * RADIUS), valid, NEG)
    zeros = jnp.zeros((tile, globals_count), F32)
    local = span - globals_count
    same[0, :, :globals_count] = zeros
    neg[0, :, :globals_count] = zeros
    same[0, :, globals_count:] = alike[:tile, :local]
    neg[0, :, globals_count:] = barred[:tile, :local]
    same[1, :, :local] = alike[tile:, tile:]
    neg[1, :, :local] = barred[tile:, tile:]
    same[1, :, local:] = zeros
    neg[1, :, local:] = zeros

    half = half_of((tile, LANES))

    def step(pair, carry):
        for block in range(2):
            start = block * (globals_count + tile)
            q = queries[pair, block * tile : (block + 1) * tile, :]
            k = keys[pair, start : start + span, :]
            v = vals[pair, start : start + span, :]
            out = jnp.zeros((tile, LANES), F32)
            for head in range(2):
                query = jnp.where(half == head, q, jnp.zeros_like(q))
                boost = bias[layer_no, 2 * pair + head]
                scores = dot_nt(query, k) + (same[block] * boost + neg[block])
                top = jnp.max(scores, axis=-1, keepdims=True)
                probs = jnp.exp(scores - top)
                total = jnp.sum(probs, axis=-1, keepdims=True)
                out = jnp.where(half == head, dot(probs.astype(BF16), v) / total, out)
            mixed[pair, block * tile : (block + 1) * tile, :] = out.astype(BF16)
        return carry

    lax.fori_loop(0, pairs, step, 0)


def fill_rows(normed_parts, w_ref, pairs, globals_count, keys, vals):
    at = globals_count
    for normed in normed_parts:
        count = normed.shape[0]

        def put(tile, part, at=at, count=count):
            ref = keys if tile < 2 * pairs else vals
            ref[tile % pairs, at : at + count, :] = part

        project(normed, w_ref, pairs, 2 * pairs, put)
        at += count


def local_first(
    bias, tokens, low, high, seg_lo, seg, seg_hi, gproj, w_qkv, w_out, gain, next_gain,
    next_w, stream_out, normed_out, kv_out, queries, keys, vals, same, neg, mixed,
):
    pairs = queries.shape[0]
    globals_count = gproj.shape[1]
    scale = jnp.asarray(0.125, BF16)
    parts = [norm_rows(ref[...].astype(F32), gain[...]) for ref in (low, tokens, high)]

    def put_q(tile, part):
        queries[tile] = part * scale

    project(parts[1], w_qkv, 0, pairs, put_q)
    fill_rows(parts, w_qkv, pairs, globals_count, keys, vals)
    attend(bias, 0, gproj, seg_lo, seg, seg_hi, queries, keys, vals, same, neg, mixed)
    stream = tokens[...].astype(F32)
    for pair in range(pairs):
        stream = stream + dot(mixed[pair], w_out[pair * LANES : (pair + 1) * LANES, :])
    stream_out[...] = stream
    normed = norm_rows(stream, next_gain[...])
    normed_out[...] = normed

    def put_kv(tile, part):
        kv_out[tile - pairs] = part

    project(normed, next_w, pairs, 2 * pairs, put_kv)


def local_second(
    bias, normed, low, high, seg_lo, seg, seg_hi, gproj, w_qkv, w_out, stream, kv,
    out, queries, keys, vals, same, neg, mixed,
):
    pairs = queries.shape[0]
    globals_count = gproj.shape[1]
    rows = normed.shape[0]
    scale = jnp.asarray(0.125, BF16)

    def put_q(tile, part):
        queries[tile] = part * scale

    project(normed[...], w_qkv, 0, pairs, put_q)
    at = globals_count
    fill_rows([low[...]], w_qkv, pairs, at, keys, vals)
    fill_rows([high[...]], w_qkv, pairs, at + low.shape[0] + rows, keys, vals)
    for pair in range(pairs):
        keys[pair, at + RADIUS : at + RADIUS + rows, :] = kv[pair]
        vals[pair, at + RADIUS : at + RADIUS + rows, :] = kv[pairs + pair]
    attend(bias, 1, gproj, seg_lo, seg, seg_hi, queries, keys, vals, same, neg, mixed)
    total = stream[...]
    for pair in range(pairs):
        total = total + dot(mixed[pair], w_out[pair * LANES : (pair + 1) * LANES, :])
    out[...] = total.astype(BF16)


def call(kernel, name, out_shape, in_specs, cost, scratch=()):
    return pl.pallas_call(
        kernel,
        name=name,
        out_shape=out_shape,
        in_specs=in_specs,
        out_specs=jax.tree.map(lambda _: VMEM, out_shape),
        scratch_shapes=list(scratch),
        cost_estimate=pl.CostEstimate(flops=cost, bytes_accessed=4 << 20, transcendentals=0),
        compiler_params=pltpu.CompilerParams(vmem_limit_bytes=48 << 20),
    )


def per_device(
    tokens, globals_in, seg_ids, global_table, w_qkv, w_out, gain_local, gain_global, seg_bias
):
    rows, width = tokens.shape
    globals_count = globals_in.shape[0]
    shard = lax.axis_index("seq")
    shards = lax.axis_size("seq")
    pairs = width // LANES
    groups = globals_count // 8
    forward = [(i, i + 1) for i in range(shards - 1)]
    backward = [(i + 1, i) for i in range(shards - 1)]

    def halo(block):
        return lax.ppermute(block, "seq", forward), lax.ppermute(block, "seq", backward)

    def exchange(block):
        return lax.all_to_all(block, "seq", 0, 0, tiled=True)

    S = jax.ShapeDtypeStruct
    seg = seg_ids.reshape(1, rows)
    table = global_table.reshape(1, globals_count)
    where = jnp.stack([shard // groups, shard % groups]).astype(jnp.int32)
    payload_shape = S((pairs, groups, 16, LANES), BF16)
    gproj_shape = S((3 * pairs, globals_count, LANES), BF16)
    kv_shape = S((2 * pairs, rows, LANES), BF16)
    scratch = (
        pltpu.VMEM((pairs, rows, LANES), BF16),
        pltpu.VMEM((pairs, rows + 2 * RADIUS + 2 * globals_count, LANES), BF16),
        pltpu.VMEM((pairs, rows + 2 * RADIUS + 2 * globals_count, LANES), BF16),
        pltpu.VMEM((2, rows // 2, rows // 2 + 2 * RADIUS + globals_count), F32),
        pltpu.VMEM((2, rows // 2, rows // 2 + 2 * RADIUS + globals_count), F32),
        pltpu.VMEM((pairs, rows, LANES), BF16),
    )

    def combine(payload, gproj):
        parts = exchange(payload.reshape(shards, 16, LANES))
        mix = call(
            combine_kernel, "combine", S((shards, 8, LANES), BF16), [SMEM, VMEM, VMEM], 1 << 28
        )(where, parts, gproj)
        return exchange(mix).reshape(pairs, globals_count, LANES)

    tok_lo, tok_hi = halo(tokens)
    seg_lo, seg_hi = halo(seg)
    payload, gproj, _ = call(
        first_kernel, "parts_first", (payload_shape, gproj_shape, kv_shape), [VMEM] * 7, 1 << 30
    )(tokens, globals_in, seg, table, gain_local[0:1], gain_global[0:1], w_qkv[0])
    mix = combine(payload, gproj)
    stream, normed, kv = call(
        local_first,
        "local_first",
        (S((rows, width), F32), S((rows, width), BF16), kv_shape),
        [SMEM] + [VMEM] * 12,
        6 << 30,
        scratch,
    )(
        seg_bias, tokens, tok_lo, tok_hi, seg_lo, seg, seg_hi, gproj, w_qkv[0], w_out[0],
        gain_local[0:1], gain_local[1:2], w_qkv[1],
    )
    low, high = halo(normed)
    payload, gproj, gstate = call(
        second_kernel,
        "parts_second",
        (payload_shape, gproj_shape, S((globals_count, width), F32)),
        [VMEM] * 8,
        1 << 30,
    )(mix, globals_in, seg, table, gain_global[1:2], w_out[0], w_qkv[1], kv)
    mix = combine(payload, gproj)
    local_out = call(
        local_second, "local_second", S((rows, width), BF16), [SMEM] + [VMEM] * 11, 6 << 30,
        scratch,
    )(
        seg_bias, normed, low, high, seg_lo, seg, seg_hi, gproj, w_qkv[1], w_out[1], stream, kv
    )
    global_out = call(
        last_kernel, "last", S((globals_count, width), BF16), [VMEM] * 3, 1 << 28
    )(mix, gstate, w_out[1])
    return local_out, global_out


def solution(mesh):
    return jax.shard_map(
        per_device,
        mesh=mesh,
        in_specs=(
            P(("dp", "seq"), None),
            P("dp", None),
            P(("dp", "seq")),
            P("dp"),
            P(),
            P(),
            P(),
            P(),
            P(),
        ),
        out_specs=(P(("dp", "seq"), None), P("dp", None)),
        check_vma=False,
    )
```
